32 devices in a mesh: sec: 2 (over core), dev: 16 (over z, y, x).
Axes of the slice: x: 2, y: 2, z: 4, core: 2. Of those that a mesh axis runs over, the one named last changes fastest.
Arguments:
- tokens: bfloat16 [512, 3584], P(('sec', 'dev')), may hold values from -6 to 6
- routes: int32 [512, 8], P(('sec', 'dev')), may hold values from 0 to 31, all different within a row; in each aligned block of 16 rows (0 to 15, 16 to 31, ...) at most 8 rows name the same one
- gate_num: int32 [512, 8], P(('sec', 'dev')), may hold values from 1 to 32
- w_gate: bfloat16 [32, 3584, 1024], P(('sec', 'dev')), may hold values from -0.09375 to 0.09375
- w_up: bfloat16 [32, 3584, 1024], P(('sec', 'dev')), may hold values from -0.09375 to 0.09375
- w_down: bfloat16 [32, 1024, 3584], P(('sec', 'dev')), may hold values from -0.1875 to 0.1875
- attn_gain: float32 [3584], replicated, may hold values from 0.25 to 1.75
- w_latent: bfloat16 [3584, 576], P('dev'), may hold values from -0.09375 to 0.09375
- kv_gain: float32 [512], replicated, may hold values from 0.25 to 1.75
- queries: bfloat16 [512, 64, 576], P(('sec', 'dev')), may hold values from -9 to 9
- cache_pool: bfloat16 [1024, 64, 576], P(('sec', 'dev')), may hold values from -4 to 4
- block_table: int32 [512, 4], P(('sec', 'dev')), may hold values from 0 to 31
- lengths: int32 [32, 16], P(('sec', 'dev')), may hold values from 1 to 256, 2048 in all within a row
Outputs:
- layer_out: bfloat16 [512, 3584], P(('sec', 'dev'))
- new_latent: bfloat16 [512, 576], P(('sec', 'dev'))
- context: bfloat16 [512, 32768], P(('sec', 'dev'))
The draws below stay inside these ranges and needn't reach their ends.
Inputs may be any that keep to these rules, and one draw needn't show every extreme that they name: `routes`: in each aligned block of 16 rows (the rows of one device) no expert is named by more than 8 rows. `block_table`: each device's rows point only into that device's 32 pages; pages may be shared by rows. The 16 lengths of one device add up to 2048.
All inputs are finite; a program needn't handle non-finite values.
Results may differ from the reference program's by a relative error of at most 0.0064.
Values may be sent and summed in bfloat16 or wider, within the bound.
No kernel may reach another device: no remote copies, remote signals or barrier semaphores. Data moves between devices by JAX's collectives and lax.ppermute only.
A program may use at most 128 MiB of HBM per device.

```python
import math
import jax
import jax.numpy as jnp
import numpy as np
from jax import lax

D = 3584
HID = 1024
HEADS = 64
LAT = 512
ROPE = 64
TOP = 8
GATE_DEN = 32
PAGE = 64
MAXP = 4
POOL = 32
TOK_DEV = 16
KDIM = 576
MAXLEN = 256
EXPERTS = 32
CAP = 8
TOKENS = 512
POOL_ALL = 1024
N_SEC = 2
N_DEV = 16


def draw_queries(key, part):
    base = jax.random.truncated_normal(jax.random.fold_in(key, 11), -4.0, 4.0, (TOKENS, HEADS, LAT + ROPE), jnp.float32)
    return base.astype(jnp.bfloat16)


def draw_cache_pool(key, part):
    shape = (POOL_ALL, PAGE, LAT + ROPE)
    base = jax.random.truncated_normal(jax.random.fold_in(key, 21), -4.0, 4.0, shape, jnp.float32)
    return base.astype(jnp.bfloat16)


def plant(drawn, own_key, smallest, largest):
    index_at = [jax.random.randint(jax.random.fold_in(own_key, axis), (), 0, length) for axis, length in enumerate(drawn.shape)]
    widest = drawn.shape.index(max(drawn.shape))
    next_to = index_at[:widest] + [(index_at[widest] + 1) % drawn.shape[widest]] + index_at[widest + 1:]
    return drawn.at[tuple(index_at)].set(smallest).at[tuple(next_to)].set(largest)


def steps_of(stream_key, dims, pieces, least, largest):
    loudness, own = 1.0, jax.random.fold_in(stream_key, 6)
    for dim, shards_of in pieces:
        heights = jnp.exp(jax.random.uniform(jax.random.fold_in(own, dim), (shards_of,), jnp.float32, least / len(pieces), largest / len(pieces)))
        loudness = loudness * jnp.repeat(heights, dims[dim] // shards_of).reshape([-1 if axis == dim else 1 for axis in range(len(dims))])
    return loudness


def length_profile(number_of, total, limit, lean):
    weights = [(1 << 20) // math.isqrt(standing ** lean) + 1 for standing in range(2, number_of + 1)]
    spare, given = total - limit - (number_of - 1), [1] * (number_of - 1)
    while spare > 0:
        movable = [i for i in range(number_of - 1) if given[i] < limit]
        mass, left = sum([weights[i] for i in movable]), spare
        for i in movable:
            extra = min(limit - given[i], max(1, left * weights[i] // mass), spare)
            given[i] = given[i] + extra
            spare = spare - extra
    return np.array([limit] + given)


def ragged(stream_key, count, total, reach, slope):
    if count == 2:
        one = jax.random.randint(stream_key, (), max(1, total - reach), min(reach, total - 1) + 1)
        return jnp.stack([one, total - one])
    sizes = jnp.asarray(length_profile(count, total, reach, slope), jnp.int32)
    couples = (count - 1) // 2
    donor, taker = sizes[1:1 + 2 * couples:2], sizes[2:2 + 2 * couples:2]
    margin = jnp.minimum(donor - 1, reach - taker)
    passed = jax.random.randint(jax.random.fold_in(stream_key, 1), (couples,), 0, 1 << 20) % (margin + 1)
    sizes = sizes.at[1:1 + 2 * couples:2].set(donor - passed).at[2:2 + 2 * couples:2].set(taker + passed)
    return sizes[jax.random.permutation(jax.random.fold_in(stream_key, 2), count)]


def assign_block(own_key, own, number, rows, count, top, bound, slope):
    order = jax.random.permutation(own_key, count)
    heavy_load, usual = shares(count, rows * top, bound, slope, True), shares(count, rows * top, bound, slope, False)
    places = jnp.arange(count)

    def named(sizes, offset_by):
        used = int((sizes > 0).sum())
        fixed = max(1, used // 4)
        passed = fixed + (places - fixed + offset_by * (used - fixed)) % max(1, count - fixed)
        return jnp.zeros((count,), jnp.int32).at[order[jnp.where(places < fixed, places, passed)]].set(jnp.asarray(sizes, jnp.int32))

    sizes = jnp.where(number % 4 == 0, named(heavy_load, number // 4), named(usual, number - number // 4 - 1))
    mixed = jax.random.permutation(jax.random.fold_in(own, 3), count)
    source_of, taker = mixed[0:count // 2 * 2:2], mixed[1:count // 2 * 2:2]
    room = jnp.minimum(sizes[source_of] - 1, bound - sizes[taker]) // 2
    room = jnp.where((source_of == order[0]) | (taker == order[0]) | (sizes[taker] == 0), 0, jnp.maximum(room, 0))
    passed = jax.random.randint(jax.random.fold_in(own, 4), (count // 2,), 0, 1 << 20) % (room + 1)
    sizes = sizes.at[source_of].add(-passed).at[taker].add(passed)
    members = jnp.searchsorted(jnp.cumsum(sizes), jnp.arange(rows * top), side="right").astype(jnp.int32)
    listing = members.reshape(top, rows).T
    listing = listing[jax.random.permutation(jax.random.fold_in(own, 1), rows)]
    offset_by = jax.random.randint(jax.random.fold_in(own, 2), (rows, 1), 0, top)
    return jnp.take_along_axis(listing, (jnp.arange(top)[None, :] + offset_by) % top, axis=1)


def shares(amount, total, bound, lean, full):
    weights = [(1 << 20) // math.isqrt(standing ** lean) + 1 for standing in range(1, amount + 1)]
    largest = bound if full else min(bound, max(-(-total // amount), total * weights[0] // sum(weights)))
    least = 1 if total - largest >= amount - 1 else 0
    holding, spare = [largest] + [least] * (amount - 1), total - largest - least * (amount - 1)
    while spare > 0:
        candidates = [i for i in range(1, amount) if holding[i] < largest] or [i for i in range(1, amount) if holding[i] < bound]
        whole, left = sum([weights[i] for i in candidates]), spare
        for i in candidates:
            extra = min(bound - holding[i], max(1, left * weights[i] // whole), spare)
            holding[i] = holding[i] + extra
            spare = spare - extra
    return np.array(holding)


def scatter_about(rng, shape, scale, bound, shards=(), kind=jnp.bfloat16):
    level = steps_of(rng, shape, shards, -0.22, 0.18) if shards else 1.0
    array = jax.random.normal(rng, shape, jnp.float32) * scale * level
    return jnp.minimum(jnp.maximum(array, -bound), bound).astype(kind)


def setup_inputs(seed: int = 0) -> dict:
    seeds = jax.random.split(jax.random.key(seed), 14)
    tokens = scatter_about(seeds[0], (TOKENS, D), 1.0, 6.0, ((0, 32),))
    routes_keys = jax.random.split(jax.random.fold_in(seeds[1], 1), TOKENS // TOK_DEV)
    routes_turns = jax.random.permutation(jax.random.fold_in(seeds[1], 3), TOKENS // TOK_DEV)
    routes = jax.vmap(lambda own, number: assign_block(jax.random.fold_in(seeds[1], 2), own, number, TOK_DEV, EXPERTS, TOP, CAP, 2))(routes_keys, routes_turns).reshape((TOKENS, TOP))
    gate_num = plant(jax.random.randint(seeds[2], (TOKENS, TOP), 1, 33), jax.random.fold_in(seeds[2], 1), 1, 32).astype(jnp.int32)
    w_gate = scatter_about(seeds[3], (EXPERTS, D, HID), D ** -0.5, 0.09375, ((0, 32),))
    w_up = scatter_about(seeds[4], (EXPERTS, D, HID), D ** -0.5, 0.09375, ((0, 32),))
    w_down = scatter_about(seeds[5], (EXPERTS, HID, D), HID ** -0.5, 0.1875, ((0, 32),))
    attn_gain = jnp.clip(1.0 + 0.15 * jax.random.normal(seeds[6], (D,), jnp.float32), 0.25, 1.75)
    w_latent = scatter_about(seeds[7], (D, KDIM), D ** -0.5, 0.09375, ((0, 16),))
    kv_gain = jnp.clip(1.0 + 0.15 * jax.random.normal(seeds[8], (LAT,), jnp.float32), 0.25, 1.75)
    queries = draw_queries(jax.random.fold_in(seeds[13], 71), 0)
    cache_pool = draw_cache_pool(jax.random.fold_in(seeds[13], 71), 0)
    block_table = plant(jax.random.randint(seeds[11], (TOKENS, MAXP), 0, POOL), jax.random.fold_in(seeds[11], 1), 0, POOL - 1).astype(jnp.int32)
    lengths = jax.vmap(lambda own: ragged(own, TOK_DEV, TOK_DEV * MAXLEN // 2, MAXLEN, 2))(jax.random.split(seeds[12], (N_SEC * N_DEV))).reshape((N_SEC * N_DEV, TOK_DEV)).astype(jnp.int32)
    return {"tokens": tokens, "routes": routes, "gate_num": gate_num, "w_gate": w_gate, "w_up": w_up, "w_down": w_down, "attn_gain": attn_gain, "w_latent": w_latent, "kv_gain": kv_gain, "queries": queries, "cache_pool": cache_pool, "block_table": block_table, "lengths": lengths}


score_scale = 192.0 ** (-0.5)
norm_eps = 1e-06

def slot_numbers(expert_rows):
    onehot = (expert_rows[:, None] == jnp.arange(EXPERTS, dtype=jnp.int32)[None, :]).astype(jnp.int32)
    before = jnp.cumsum(onehot, axis=0) - onehot
    return lax.optimization_barrier(jnp.sum(before * onehot, axis=1)).astype(jnp.int32)

def rms_scale(values, gain):
    mean_square = lax.optimization_barrier(jnp.mean(values * values, axis=-1, keepdims=True))
    return values * lax.rsqrt(mean_square + norm_eps) * gain.astype(jnp.float32)

def expert_apply(rows, gates, gate_proj, up_proj, down_proj):
    gate_part = jnp.dot(rows, gate_proj, preferred_element_type=jnp.float32)
    up_part = jnp.dot(rows, up_proj, preferred_element_type=jnp.float32)
    hidden = (jax.nn.silu(gate_part) * up_part).astype(jnp.bfloat16)
    result = jnp.dot(hidden, down_proj, preferred_element_type=jnp.float32)
    return (result * gates.astype(jnp.float32)[:, None]).astype(jnp.bfloat16)

def attend(queries, key_rows, row_lengths):
    span = key_rows.shape[1] - 1
    kept = jnp.concatenate([jnp.arange(span, dtype=jnp.int32)[None, :] < row_lengths[:, None], jnp.ones((key_rows.shape[0], 1), dtype=bool)], axis=1)
    scores = jnp.einsum('thk,tpk->thp', queries.astype(jnp.float32), key_rows.astype(jnp.float32)) * score_scale
    scores = jnp.where(kept[:, None, :], scores, -1e+30)
    top_score = lax.optimization_barrier(jnp.max(scores, axis=2, keepdims=True))
    raised = jnp.exp(scores - top_score)
    probs = (raised / lax.optimization_barrier(jnp.sum(raised, axis=2, keepdims=True))).astype(jnp.bfloat16)
    values = key_rows[:, :, :LAT]
    mixed = jnp.einsum('thp,tpl->thl', probs.astype(jnp.float32), values.astype(jnp.float32))
    return mixed.astype(jnp.bfloat16).reshape(key_rows.shape[0], HEADS * LAT)

def reference(tokens, routes, gate_num, w_gate, w_up, w_down, attn_gain, w_latent, kv_gain, queries, cache_pool, block_table, lengths):
    device_count = N_SEC * N_DEV
    rows_dev = TOK_DEV * TOP
    expert_rows = routes.reshape(device_count, rows_dev).astype(jnp.int32)
    slots = jax.vmap(slot_numbers)(expert_rows)
    source = jnp.arange(device_count, dtype=jnp.int32)[:, None]
    column = (source * CAP + slots).astype(jnp.int32)
    row_ids = jnp.arange(device_count * rows_dev, dtype=jnp.int32).reshape(device_count, rows_dev)
    table = jnp.zeros((EXPERTS, device_count * CAP), jnp.int32).at[expert_rows, column].set(row_ids + 1)
    gate_flat = gate_num.reshape(-1).astype(jnp.float32) / GATE_DEN

    def one_expert(packed):
        filled, gate_proj, up_proj, down_proj = packed
        live_slot = filled > 0
        source_row = jnp.maximum(filled - 1, 0)
        rows = jnp.where(live_slot[:, None], tokens[source_row // TOP], jnp.zeros((), tokens.dtype))
        gates = jnp.where(live_slot, gate_flat[source_row], 0.0)
        return expert_apply(rows, gates, gate_proj, up_proj, down_proj)
    outputs = lax.map(one_expert, (table, w_gate, w_up, w_down))
    picked = outputs[expert_rows.reshape(-1), column.reshape(-1)]
    moe = lax.optimization_barrier(jnp.sum(picked.astype(jnp.float32).reshape(TOKENS, TOP, D), axis=1))
    layer_out = (tokens.astype(jnp.float32) + moe).astype(jnp.bfloat16)
    normed = rms_scale(layer_out.astype(jnp.float32), attn_gain).astype(jnp.bfloat16)
    latent_full = jnp.dot(normed, w_latent, preferred_element_type=jnp.float32)
    latent = rms_scale(latent_full[:, :LAT], kv_gain)
    new_latent = jnp.concatenate([latent, latent_full[:, LAT:]], axis=1).astype(jnp.bfloat16)
    pool = cache_pool.reshape(device_count, POOL, PAGE, KDIM)

    def one_device(packed):
        device_queries, pages, table_rows, row_lengths, own = packed
        key_rows = pages[table_rows].reshape(TOK_DEV, MAXLEN, KDIM)
        key_rows = jnp.concatenate([key_rows, own[:, None, :]], axis=1)
        return attend(device_queries, key_rows, row_lengths)
    context = lax.map(one_device, (queries.reshape(device_count, TOK_DEV, HEADS, KDIM), pool, block_table.reshape(device_count, TOK_DEV, MAXP).astype(jnp.int32), lengths.astype(jnp.int32), new_latent.reshape(device_count, TOK_DEV, KDIM)))
    context = context.reshape(TOKENS, HEADS * LAT)
    return (layer_out, new_latent, context)
```

```python
import functools
import math

import jax
import jax.numpy as jnp
from jax import lax
from jax.experimental import pallas as pl
from jax.experimental.pallas import tpu as pltpu
from jax.sharding import PartitionSpec as P

GATE_DEN = 32
LANES = 128

score_scale = 192.0 ** (-0.5)
norm_eps = 1e-06
f32 = jnp.float32
bf16 = jnp.bfloat16
VM = pl.BlockSpec(memory_space=pltpu.VMEM)
SM = pl.BlockSpec(memory_space=pltpu.SMEM)
ANY = pl.BlockSpec(memory_space=pl.ANY)


def dims_of(chips):
    column = 4
    side = math.isqrt(max(chips // column, 1))
    if column * side * side == chips:
        return column, side
    return chips, 1


class Routes:
    def __init__(self, sections, chips):
        self.sections, self.chips = sections, chips
        self.column, self.side = dims_of(chips)

    def hop(self, x, kind, k):
        pairs = []
        column, side = self.column, self.side
        for s in range(self.sections):
            for z in range(column):
                for p in range(side):
                    for q in range(side):
                        s2, z2, p2, q2 = s, z, p, q
                        if kind == "sec":
                            s2 = (s + k) % self.sections
                        elif kind == "col":
                            z2 = (z + k) % column
                        elif (kind == "one") == (s % 2 == 0):
                            q2 = (q + k) % side
                        else:
                            p2 = (p + k) % side
                        pairs.append(
                            (
                                s * self.chips + (z * side + p) * side + q,
                                s2 * self.chips + (z2 * side + p2) * side + q2,
                            )
                        )
        return lax.ppermute(x, ("sec", "dev"), pairs)

    def size(self, kind):
        return {"sec": self.sections, "col": self.column}.get(kind, self.side)

    def gather(self, x, kind):
        return [x] + [self.hop(x, kind, k) for k in range(1, self.size(kind))]


def pick_rows(tail, expert, fanout, tok_rows, capacity):
    rows = tail.shape[0]
    slots = rows // tok_rows * capacity
    lane = lax.broadcasted_iota(jnp.int32, tail.shape, 1)
    hit = jnp.where((tail == expert) & (lane < fanout), 1.0, 0.0)
    named = jnp.broadcast_to(jnp.sum(hit, axis=1, keepdims=True), (rows, slots))
    row = lax.broadcasted_iota(jnp.int32, (rows, slots), 0)
    within = row & (tok_rows - 1)
    block = lax.shift_right_logical(row, tok_rows.bit_length() - 1)
    count = named
    shift = 1
    while shift < tok_rows:
        count = count + jnp.where(within >= shift, pltpu.roll(count, shift, 0), 0.0)
        shift *= 2
    slot = block * capacity + count.astype(jnp.int32) - 1
    column = lax.broadcasted_iota(jnp.int32, (rows, slots), 1)
    return jnp.where((slot == column) & (named > 0), 1.0, 0.0).astype(bf16)


def slot_gates(tail, expert, fanout):
    lane = lax.broadcasted_iota(jnp.int32, tail.shape, 1)
    hit = jnp.where((tail == expert) & (lane < fanout), 1.0, 0.0)
    return jnp.sum(pltpu.roll(hit, fanout, 1) * tail, axis=1, keepdims=True) / GATE_DEN


def dot_t(a, b):
    return lax.dot_general(a, b, (((0,), (0,)), ((), ())), preferred_element_type=f32)


def expert_kernel(cfg, *refs):
    sections, fanout, tok_rows, capacity, hid_tile, out_tile = cfg
    ids = refs[0]
    first = refs[1 : 1 + sections]
    second = refs[1 + sections : 1 + 2 * sections]
    wg_hbm, wu_hbm, wd_hbm = refs[1 + 2 * sections : 4 + 2 * sections]
    rest = refs[4 + 2 * sections :]
    outs_first, outs_second = rest[:sections], rest[sections : 2 * sections]
    pick_ref, wg_v, wu_v, wd_v, xc_v, h_v, gate_v, sem = rest[2 * sections :]
    hid_steps, out_steps = wg_v.shape[0], wd_v.shape[0]
    copies = []
    for j in range(hid_steps):
        part = pl.ds(j * hid_tile, hid_tile)
        copies.append(pltpu.make_async_copy(wg_hbm.at[0, :, part], wg_v.at[j], sem.at[2 * j]))
        copies.append(pltpu.make_async_copy(wu_hbm.at[0, :, part], wu_v.at[j], sem.at[2 * j + 1]))
    for j in range(out_steps):
        part = pl.ds(j * out_tile, out_tile)
        copies.append(
            pltpu.make_async_copy(wd_hbm.at[0, :, part], wd_v.at[j], sem.at[2 * hid_steps + j])
        )
    for c in copies:
        c.start()
    wide = first[0].shape[1]
    slots = pick_ref.shape[1] // sections
    mine = ids[0].astype(f32)
    for g in range(sections):
        tail = second[g][:, second[g].shape[1] - LANES :].astype(f32)
        pick = pick_rows(tail, mine, fanout, tok_rows, capacity)
        rows = pl.ds(g * slots, slots)
        xc_v[rows, :wide] = dot_t(pick, first[g][...]).astype(bf16)
        got = dot_t(pick, second[g][...])
        narrow = got.shape[1] - LANES
        xc_v[rows, wide:] = got[:, :narrow].astype(bf16)
        gate_v[rows, :] = jnp.broadcast_to(
            slot_gates(got[:, narrow:], mine, fanout), (slots, LANES)
        )
        if g == 0:
            pick_ref[:, :slots] = pick
            for k in range(1, sections):
                pick_ref[:, k * slots : (k + 1) * slots] = pick_rows(
                    tail, ids[k].astype(f32), fanout, tok_rows, capacity
                )
    xc = xc_v[...]
    for j in range(hid_steps):
        copies[2 * j].wait()
        gate = jnp.dot(xc, wg_v[j], preferred_element_type=f32)
        copies[2 * j + 1].wait()
        up = jnp.dot(xc, wu_v[j], preferred_element_type=f32)
        h_v[:, j * hid_tile : (j + 1) * hid_tile] = (
            gate / (1.0 + jnp.exp(-gate)) * up
        ).astype(bf16)
    scale = gate_v[:, :1]
    h = h_v[...]
    per = wide // out_tile
    for j in range(out_steps):
        copies[2 * hid_steps + j].wait()
        res = (jnp.dot(h, wd_v[j], preferred_element_type=f32) * scale).astype(bf16)
        outs = outs_first if j < per else outs_second
        at = (j % per) * out_tile
        for g in range(sections):
            outs[g][:, at : at + out_tile] = res[g * slots : (g + 1) * slots]


def combine_kernel(pick_ref, *refs):
    sections = len(refs) - 1
    out = refs[-1]
    slots = pick_ref.shape[1] // sections
    total = None
    for k in range(sections):
        part = jnp.dot(
            pick_ref[:, k * slots : (k + 1) * slots], refs[k][...], preferred_element_type=f32
        )
        total = part if total is None else total + part
    out[...] = total.astype(bf16)


def attend_kernel(table, lengths, q_ref, pool_ref, acc_ref, top_ref, sum_ref, key_v):
    tokens, heads, _ = q_ref.shape
    _, page, _ = pool_ref.shape
    pages = key_v.shape[0] // page
    lat = acc_ref.shape[0] * LANES

    def one(t, carry):
        for i in range(pages):
            key_v[i * page : (i + 1) * page, :] = pool_ref[table[t, i]]
        keys = key_v[...]
        scores = (
            lax.dot_general(
                q_ref[t], keys, (((1,), (1,)), ((), ())), preferred_element_type=f32
            )
            * score_scale
        )
        at = lax.broadcasted_iota(jnp.int32, scores.shape, 1)
        scores = jnp.where(at < lengths[0, t], scores, -1e30)
        top = jnp.max(scores, axis=1, keepdims=True)
        raised = jnp.exp(scores - top)
        total = jnp.sum(raised, axis=1, keepdims=True)
        mixed = jnp.dot(raised.astype(bf16), keys[:, :lat], preferred_element_type=f32)
        rows = pl.ds(t, heads, stride=tokens)
        for c in range(lat // LANES):
            acc_ref[c, rows, :] = mixed[:, c * LANES : (c + 1) * LANES]
        top_ref[rows, :] = jnp.broadcast_to(top, (heads, LANES))
        sum_ref[rows, :] = jnp.broadcast_to(total, (heads, LANES))
        return carry

    lax.fori_loop(0, tokens, one, 0)


def final_kernel(parts, *refs):
    first, second = refs[:parts], refs[parts : 2 * parts]
    tokens, gain, w, kv_gain, q_ref, acc, top, total = refs[2 * parts : 2 * parts + 8]
    layer_ref, latent_ref, context_ref = refs[2 * parts + 8 : 2 * parts + 11]
    b_a, b_p = refs[2 * parts + 11 :]
    rows = tokens.shape[0]
    lat_width = kv_gain.shape[1]

    def sums(refs_):
        s = refs_[0][...].astype(f32)
        for r in refs_[1:]:
            s = s + r[...].astype(f32)
        return s

    moe = jnp.concatenate([sums(first), sums(second)], axis=1)
    layer = (tokens[...].astype(f32) + moe).astype(bf16)
    layer_ref[...] = layer
    values = layer.astype(f32)
    mean_square = jnp.mean(values * values, axis=1, keepdims=True)
    normed = (values * lax.rsqrt(mean_square + norm_eps) * gain[...]).astype(bf16)
    full = jnp.dot(normed, w[...], preferred_element_type=f32)
    lat = full[:, :lat_width]
    mean_square = jnp.mean(lat * lat, axis=1, keepdims=True)
    lat = (lat * lax.rsqrt(mean_square + norm_eps) * kv_gain[...]).astype(bf16)
    new = jnp.concatenate([lat, full[:, lat_width:].astype(bf16)], axis=1)
    latent_ref[...] = new
    every = lax.dot_general(
        q_ref[...], new, (((1,), (1,)), ((), ())), preferred_element_type=f32
    )
    at = lax.broadcasted_iota(jnp.int32, every.shape, 1)
    row = lax.broadcasted_iota(jnp.int32, every.shape, 0)
    own = jnp.sum(
        jnp.where(at == (row & (rows - 1)), every, 0.0), axis=1, keepdims=True
    ) * score_scale
    own = jnp.broadcast_to(own, top.shape)
    best = jnp.maximum(top[...], own)
    old = jnp.exp(top[...] - best)
    fresh = jnp.exp(own - best)
    inverse = 1.0 / (total[...] * old + fresh)
    b_a[...] = old * inverse
    b_p[...] = fresh * inverse
    value = lat.astype(f32)
    for h in range(acc.shape[1] // rows):
        span = slice(h * rows, (h + 1) * rows)
        a, p = b_a[span, :], b_p[span, :]
        for c in range(lat_width // LANES):
            cols = slice(c * LANES, (c + 1) * LANES)
            context_ref[:, h * lat_width + c * LANES : h * lat_width + (c + 1) * LANES] = (
                acc[c, span, :] * a + value[:, cols] * p
            ).astype(bf16)


def per_device(
    tokens,
    routes,
    gate_num,
    w_gate,
    w_up,
    w_down,
    attn_gain,
    w_latent,
    kv_gain,
    queries,
    cache_pool,
    block_table,
    lengths,
):
    sections = lax.axis_size("sec")
    chips = lax.axis_size("dev")
    experts = sections * chips
    tok_rows, width = tokens.shape
    fanout = routes.shape[1]
    capacity = 2 * tok_rows * fanout // experts
    hidden = w_gate.shape[2]
    heads, kdim = queries.shape[1:]
    lat_width = kv_gain.shape[0]
    net = Routes(sections, chips)
    sec, dev = lax.axis_index("sec"), lax.axis_index("dev")
    wide = width // 2
    rows_sec = tok_rows * chips
    slots = capacity * chips

    tail = jnp.pad(
        jnp.concatenate([routes, gate_num], axis=1).astype(bf16),
        ((0, 0), (0, LANES - 2 * fanout)),
    )
    chunks = [tokens[:, :wide], jnp.concatenate([tokens[:, wide:], tail], axis=1)]
    gathered = []
    for x in chunks:
        for kind in ("col", "one", "two"):
            x = jnp.concatenate(net.gather(x, kind), axis=0)
        gathered.append(net.gather(x, "sec"))

    w_rows = w_latent.shape[0] // sections
    w_own = lax.dynamic_slice(w_latent, (sec * w_rows, 0), (w_rows, kdim))
    w_parts = w_own[None]
    for kind in ("col", "one", "two"):
        w_parts = jnp.concatenate(net.gather(w_parts, kind), axis=0)
    side = net.side
    z, p, q = dev // (side * side), dev // side % side, dev % side
    w_grid = jnp.zeros((chips, sections, w_rows, kdim), bf16)
    w_secs = net.gather(w_parts, "sec")
    for k in range(sections):
        owner = (sec - k) % sections
        for i in range(chips):
            kz, k1, k2 = i % net.column, i // net.column % side, i // net.column // side
            even = owner % 2 == 0
            kp, kq = jnp.where(even, k2, k1), jnp.where(even, k1, k2)
            at = (((z - kz) % net.column) * side + (p - kp) % side) * side + (q - kq) % side
            w_grid = lax.dynamic_update_slice(w_grid, w_secs[k][i][None, None], (at, owner, 0, 0))
    w_all = w_grid.reshape(width, kdim)

    q_heads = jnp.swapaxes(queries, 0, 1).reshape(heads * tok_rows, kdim)
    acc, top, total = pl.pallas_call(
        attend_kernel,
        out_shape=(
            jax.ShapeDtypeStruct((lat_width // LANES, heads * tok_rows, LANES), f32),
            jax.ShapeDtypeStruct((heads * tok_rows, LANES), f32),
            jax.ShapeDtypeStruct((heads * tok_rows, LANES), f32),
        ),
        in_specs=[SM, SM, VM, VM],
        out_specs=(VM, VM, VM),
        scratch_shapes=[pltpu.VMEM((block_table.shape[1] * cache_pool.shape[1], kdim), bf16)],
        cost_estimate=pl.CostEstimate(
            flops=10**9, bytes_accessed=20 * 10**6, transcendentals=10**6
        ),
        name="attend",
    )(block_table, lengths, queries, cache_pool)

    hid_tile = min(256, hidden)
    out_tile = 256 if wide % 256 == 0 else LANES
    ids = jnp.stack([(sec + k) % sections * chips + dev for k in range(sections)]).astype(jnp.int32)
    cfg = (sections, fanout, tok_rows, capacity, hid_tile, out_tile)
    results = pl.pallas_call(
        functools.partial(expert_kernel, cfg),
        out_shape=tuple(
            jax.ShapeDtypeStruct((slots, wide if i < sections else width - wide), bf16)
            for i in range(2 * sections)
        )
        + (jax.ShapeDtypeStruct((rows_sec, sections * slots), bf16),),
        in_specs=[SM] + [VM] * (2 * sections) + [ANY] * 3,
        out_specs=(VM,) * (2 * sections + 1),
        scratch_shapes=[
            pltpu.VMEM((hidden // hid_tile, width, hid_tile), bf16),
            pltpu.VMEM((hidden // hid_tile, width, hid_tile), bf16),
            pltpu.VMEM((width // out_tile, hidden, out_tile), bf16),
            pltpu.VMEM((sections * slots, width), bf16),
            pltpu.VMEM((sections * slots, hidden), bf16),
            pltpu.VMEM((sections * slots, LANES), f32),
            pltpu.SemaphoreType.DMA((2 * (hidden // hid_tile) + width // out_tile,)),
        ],
        cost_estimate=pl.CostEstimate(
            flops=6 * 10**9, bytes_accessed=25 * 10**6, transcendentals=10**6
        ),
        name="experts",
    )(ids, *gathered[0], *gathered[1], w_gate, w_up, w_down)
    pick = results[-1]

    final_parts = []
    for c in range(2):
        outs = results[c * sections : (c + 1) * sections]
        back = [net.hop(outs[k], "sec", -k) for k in range(1, sections)]
        part = pl.pallas_call(
            combine_kernel,
            out_shape=jax.ShapeDtypeStruct((rows_sec, outs[0].shape[1]), bf16),
            in_specs=[VM] * (sections + 1),
            out_specs=VM,
            cost_estimate=pl.CostEstimate(
                flops=10**8, bytes_accessed=2 * 10**6, transcendentals=0
            ),
            name="combine",
        )(pick, outs[0], *back)
        pieces = [part]
        for kind in ("two", "one"):
            n = net.size(kind)
            step = pieces[0].shape[0] // n
            cuts = [
                [x[k * step : (k + 1) * step] for x in pieces] for k in range(n)
            ]
            sent = [
                sum(y.astype(f32) for y in cuts[k]).astype(bf16) if len(pieces) > 1 else cuts[k][0]
                for k in range(n)
            ]
            pieces = cuts[0] + [net.hop(sent[k], kind, -k) for k in range(1, n)]
        n = net.column
        cuts = [[x[k * tok_rows : (k + 1) * tok_rows] for x in pieces] for k in range(n)]
        sent = [sum(y.astype(f32) for y in cuts[k]).astype(bf16) for k in range(n)]
        final_parts.append(
            [sum(y.astype(f32) for y in cuts[0])]
            + [net.hop(sent[k], "col", -k) for k in range(1, n)]
        )
    parts = len(final_parts[0])
    layer_out, new_latent, context = pl.pallas_call(
        functools.partial(final_kernel, parts),
        out_shape=(
            jax.ShapeDtypeStruct((tok_rows, width), bf16),
            jax.ShapeDtypeStruct((tok_rows, kdim), bf16),
            jax.ShapeDtypeStruct((tok_rows, heads * lat_width), bf16),
        ),
        in_specs=[VM] * (2 * parts + 8),
        out_specs=(VM, VM, VM),
        scratch_shapes=[
            pltpu.VMEM((heads * tok_rows, LANES), f32),
            pltpu.VMEM((heads * tok_rows, LANES), f32),
        ],
        cost_estimate=pl.CostEstimate(
            flops=10**8, bytes_accessed=8 * 10**6, transcendentals=10**5
        ),
        name="final",
    )(
        *final_parts[0],
        *final_parts[1],
        tokens,
        attn_gain.reshape(1, -1),
        w_all,
        kv_gain.reshape(1, -1),
        q_heads,
        acc,
        top,
        total,
    )
    return (layer_out, new_latent, context)


def solution(mesh):
    both = ("sec", "dev")
    return jax.shard_map(
        per_device,
        mesh=mesh,
        in_specs=(
            P(both, None),
            P(both, None),
            P(both, None),
            P(both, None, None),
            P(both, None, None),
            P(both, None, None),
            P(),
            P("dev", None),
            P(),
            P(both, None, None),
            P(both, None, None),
            P(both, None),
            P(both, None),
        ),
        out_specs=(P(both, None), P(both, None), P(both, None)),
        check_vma=False,
    )
```
